32 devices in a mesh: ta: 4 (over x, core), ha: 4 (over z), wa: 2 (over y).
Axes of the slice: x: 2, y: 2, z: 4, core: 2. Of those that a mesh axis runs over, the one named last changes fastest.
Arguments:
- teacher_in: bfloat16 [8, 128, 16, 192], P('ta', 'ha', 'wa'), may hold values from -3 to 3
- teacher_weights: bfloat16 [1, 2, 3, 3, 3, 192, 192], replicated, may hold values from -0.4375 to 0.4375
- student_in: bfloat16 [8, 128, 16, 128], P('ta', ('ha', 'wa')), may hold values from -6 to 6
- depth_weights: float32 [4, 3, 3, 3, 128], replicated, may hold values from -1.25 to 1.25
- point_weights: bfloat16 [4, 128, 128], replicated, may hold values from -0.5 to 0.5
- project_weight: bfloat16 [128, 192], replicated, may hold values from -0.5 to 0.5
Outputs:
- voxel_grad: bfloat16 [8, 128, 16, 128], P('ta', ('ha', 'wa'))
The draws below stay inside these ranges and needn't reach their ends.
All inputs are finite; a program needn't handle non-finite values.
Results may differ from the reference program's by a relative error of at most 0.01.
Values may be sent and summed in bfloat16 or wider, within the bound.
No kernel may reach another device: no remote copies, remote signals or barrier semaphores. Data moves between devices by JAX's collectives and lax.ppermute only.
A program may use at most 128 MiB of HBM per device.

```python
import jax
import jax.numpy as jnp
from jax import lax

CT = 192
CS = 128
BLOCKS = 1
LAYERS = 4
NT = 8
NH = 128
NW = 16


def shard_levels(stream_key, dims, pieces, low, largest):
    def one(dim, shards_of):
        draws = jax.random.uniform(jax.random.fold_in(jax.random.fold_in(stream_key, 6), dim), (shards_of,), jnp.float32, low / len(pieces), largest / len(pieces))
        return jnp.repeat(jnp.exp(draws), dims[dim] // shards_of).reshape((-1,) + (1,) * (len(dims) - dim - 1))

    level = one(*pieces[0])
    for cut in pieces[1:]:
        level = level * one(*cut)
    return level


def noise(own_key, shape, width, limit, shards=(), kind=jnp.bfloat16):
    factor_of = shard_levels(own_key, shape, shards, -0.22, 0.18) if shards else 1.0
    entries = jax.random.normal(own_key, shape, jnp.float32) * width * factor_of
    return jnp.minimum(jnp.maximum(entries, -limit), limit).astype(kind)


def setup_inputs(seed: int = 0) -> dict:
    keys = jax.random.split(jax.random.key(seed), 7)
    return {
        "teacher_in": noise(keys[0], (NT, NH, NW, CT), 0.5, 3.0, ((0, 4), (1, 4), (2, 2))),
        "teacher_weights": noise(keys[1], (BLOCKS, 2, 3, 3, 3, CT, CT), CT ** -0.5, 0.4375),
        "student_in": noise(keys[2], (NT, NH, NW, CS), 1.0, 6.0, ((0, 4), (1, 8))),
        "depth_weights": noise(keys[3], (LAYERS, 3, 3, 3, CS), 27 ** -0.5, 1.25, (), jnp.float32),
        "point_weights": noise(keys[4], (LAYERS, CS, CS), CS ** -0.5, 0.5),
        "project_weight": noise(keys[5], (CS, CT), CS ** -0.5, 0.5),
    }


def root_norm(field):
    return field * lax.rsqrt(lax.optimization_barrier(jnp.mean(field * field, axis=-1, keepdims=True)) + 1e-06)

def silu_slope(field):
    sigmoid_value = jax.nn.sigmoid(field)
    return sigmoid_value * (1.0 + field * (1.0 - sigmoid_value))

def causal_pad(field):
    return jnp.pad(field, ((2, 0), (1, 1), (1, 1), (0, 0)))

def future_pad(field):
    return jnp.pad(field, ((0, 2), (1, 1), (1, 1), (0, 0)))

def dense_conv(extended, kernel):
    frame_count = extended.shape[0] - 2
    row_count = extended.shape[1] - 2
    col_count = extended.shape[2] - 2
    channels = kernel.shape[-1]
    summed = jnp.zeros((frame_count * row_count * col_count, channels), jnp.float32)
    for step_t in range(3):
        for step_h in range(3):
            for step_w in range(3):
                tap_slice = extended[step_t:step_t + frame_count, step_h:step_h + row_count, step_w:step_w + col_count]
                summed = summed + jnp.dot(tap_slice.reshape(-1, tap_slice.shape[-1]), kernel[step_t, step_h, step_w], preferred_element_type=jnp.float32)
    return summed.reshape(frame_count, row_count, col_count, channels)

def depthwise(extended, kernel):
    frame_count = extended.shape[0] - 2
    row_count = extended.shape[1] - 2
    col_count = extended.shape[2] - 2
    summed = jnp.zeros((frame_count, row_count, col_count, kernel.shape[-1]), jnp.float32)
    for step_t in range(3):
        for step_h in range(3):
            for step_w in range(3):
                tap_slice = extended[step_t:step_t + frame_count, step_h:step_h + row_count, step_w:step_w + col_count]
                summed = summed + tap_slice.astype(jnp.float32) * kernel[step_t, step_h, step_w]
    return summed

def reference(teacher_in, teacher_weights, student_in, depth_weights, point_weights, project_weight):
    target = teacher_in
    for block_index in range(teacher_weights.shape[0]):
        current = target.astype(jnp.float32)
        active = jax.nn.silu(root_norm(current)).astype(jnp.bfloat16)
        middle = dense_conv(causal_pad(active), teacher_weights[block_index, 0])
        second = jax.nn.silu(root_norm(middle)).astype(jnp.bfloat16)
        target = (current + dense_conv(causal_pad(second), teacher_weights[block_index, 1])).astype(jnp.bfloat16)
    channels = student_in.shape[-1]
    current = student_in.astype(jnp.float32)
    stored = []
    for layer_index in range(depth_weights.shape[0]):
        active = jax.nn.silu(current).astype(jnp.bfloat16)
        spread = depthwise(causal_pad(active), depth_weights[layer_index]).astype(jnp.bfloat16)
        stored.append(current)
        mixed = jnp.dot(spread.reshape(-1, channels), point_weights[layer_index], preferred_element_type=jnp.float32)
        current = current + mixed.reshape(current.shape)
    projected = jnp.dot(current.astype(jnp.bfloat16).reshape(-1, channels), project_weight, preferred_element_type=jnp.float32)
    mismatch = (projected - target.astype(jnp.float32).reshape(projected.shape)).astype(jnp.bfloat16)
    gradient = lax.dot_general(mismatch, project_weight, (((1,), (1,)), ((), ())), preferred_element_type=jnp.float32).reshape(current.shape)
    for layer_index in reversed(range(depth_weights.shape[0])):
        backward = lax.dot_general(gradient.astype(jnp.bfloat16).reshape(-1, channels), point_weights[layer_index], (((1,), (1,)), ((), ())), preferred_element_type=jnp.float32)
        backward = backward.astype(jnp.bfloat16).reshape(current.shape)
        flipped = depth_weights[layer_index][::-1, ::-1, ::-1]
        spread_back = depthwise(future_pad(backward), flipped)
        gradient = gradient + spread_back * silu_slope(stored[layer_index])
    return gradient.astype(jnp.bfloat16)
```

```python
import functools

import jax
import jax.numpy as jnp
from jax import lax
from jax.experimental import pallas as pl
from jax.experimental.pallas import tpu as pltpu
from jax.sharding import PartitionSpec as P

FRAME_REACH = 2
TEACHER_HALO = 2
VMEM_BYTES = 56 * 1024 * 1024


def student_halos(layers):
    halos = [0] * (layers + 1)
    for layer in reversed(range(layers)):
        halos[layer] = max(layer, halos[layer + 1] + 1)
    return halos


def slot_of(source, own, slots):
    difference = source ^ own
    bits = slots.bit_length() - 1
    slot = 0
    for bit in range(bits):
        slot = slot | (((difference >> bit) & 1) << (bits - 1 - bit))
    return slot


def row_position(rows_each):
    time = lax.axis_index("ta")
    chain = lax.axis_index("ha") * lax.axis_size("wa") + lax.axis_index("wa")
    count = lax.axis_size("ta")
    part = time ^ ((chain & 1) * (count - 1))
    return time, chain, part, (chain * count + part) * rows_each


def row_mask(row, total):
    return jnp.where((row >= 0) & (row < total), 1.0, 0.0).astype(jnp.float32)


def moved(field, step):
    width = field.shape[-2]
    rolled = pltpu.roll(field, step % width, field.ndim - 2)
    column = lax.broadcasted_iota(jnp.int32, field.shape, field.ndim - 2)
    lost = 0 if step > 0 else width - 1
    return jnp.where(column == lost, 0.0, rolled)


def tap_sum(read, taps, flip):
    sides = [None, None, None]
    for step_t in range(3):
        for step_h in range(3):
            block = read(step_t, step_h)
            for step_w in range(3):
                tap = (2 - step_t, 2 - step_h, 2 - step_w) if flip else (step_t, step_h, step_w)
                term = block * taps[tap]
                sides[step_w] = term if sides[step_w] is None else sides[step_w] + term
    return sides[1] + moved(sides[0], 1) + moved(sides[2], -1)


def load_taps(depth_ref, layer):
    taps = {}
    for step_t in range(3):
        for step_h in range(3):
            for step_w in range(3):
                line = (step_t * 3 + step_h) * 3 + step_w
                taps[(step_t, step_h, step_w)] = depth_ref[layer, line : line + 1, :]
    return taps


def forward_kernel(rows_each, total_rows, halos, parts_ref, depth_ref, point_ref, *refs):
    layers = len(halos) - 1
    last_ref = refs[0]
    slope_refs = refs[1 : 1 + layers]
    state_ref, active_ref, mixed_ref = refs[1 + layers :]
    slots, own_frames, _, width, channels = parts_ref.shape
    frames = slots * own_frames
    time, _, _, first_row = row_position(rows_each)

    def start(t, carry):
        state_ref[t] = parts_ref[slot_of(t // own_frames, time, slots), t % own_frames].astype(
            jnp.float32
        )
        return carry

    lax.fori_loop(0, frames, start, 0)
    active_ref[0:FRAME_REACH] = jnp.zeros((FRAME_REACH,) + active_ref.shape[1:], jnp.float32)
    for layer in range(layers):
        halo, out_halo = halos[layer], halos[layer + 1]
        shift = halos[0] - halo
        out_rows = rows_each + 2 * out_halo

        def activate(t, carry, halo=halo, shift=shift, layer=layer):
            for row in range(rows_each + 2 * halo):
                value = state_ref[t, shift + row]
                sigma = jax.nn.sigmoid(value)
                active = (value * sigma).astype(jnp.bfloat16).astype(jnp.float32)
                active_ref[t + FRAME_REACH, shift + row] = active * row_mask(
                    first_row + row - halo, total_rows
                )
                slope_row = row - (halo - layer)
                if 0 <= slope_row < rows_each + 2 * layer:
                    slope_refs[layer][t, slope_row] = sigma * (1.0 + value * (1.0 - sigma))
            return carry

        lax.fori_loop(0, frames, activate, 0)

        def mix(t, carry, shift=shift, out_rows=out_rows, layer=layer, out_halo=out_halo):
            taps = load_taps(depth_ref, layer)
            for row in range(out_rows):
                spread = tap_sum(
                    lambda i, j, row=row: active_ref[t + i, shift + row + j], taps, False
                )
                mixed_ref[row * width : (row + 1) * width] = spread.astype(jnp.bfloat16)
            mixed = jnp.dot(
                mixed_ref[0 : out_rows * width],
                point_ref[layer],
                preferred_element_type=jnp.float32,
            ).reshape(out_rows, width, channels)
            following = state_ref[t, shift + 1 : shift + 1 + out_rows] + mixed
            if layer == layers - 1:
                last_ref[t] = following.astype(jnp.bfloat16)
            else:
                state_ref[t, shift + 1 : shift + 1 + out_rows] = following
            return carry

        if halo - out_halo == 1:
            lax.fori_loop(0, frames, mix, 0)
        else:
            inner = halo - out_halo - 1

            def mix_inner(t, carry, base=shift + inner, out_rows=out_rows, layer=layer):
                return mix(t, carry, shift=base, out_rows=out_rows, layer=layer)

            lax.fori_loop(0, frames, mix_inner, 0)


def student_forward(parts, depth_weights, point_weights, rows_each, total_rows):
    layers = depth_weights.shape[0]
    halos = student_halos(layers)
    slots, own_frames, rows, width, channels = parts.shape
    frames = slots * own_frames
    shapes = [jax.ShapeDtypeStruct((frames, rows_each, width, channels), jnp.bfloat16)]
    for layer in range(layers):
        shapes.append(
            jax.ShapeDtypeStruct((frames, rows_each + 2 * layer, width, channels), jnp.float32)
        )
    return pl.pallas_call(
        functools.partial(forward_kernel, rows_each, total_rows, halos),
        out_shape=shapes,
        scratch_shapes=[
            pltpu.VMEM((frames, rows, width, channels), jnp.float32),
            pltpu.VMEM((frames + FRAME_REACH, rows, width, channels), jnp.float32),
            pltpu.VMEM((rows * width, channels), jnp.bfloat16),
        ],
        compiler_params=pltpu.CompilerParams(vmem_limit_bytes=VMEM_BYTES),
        name="student_forward",
    )(parts, depth_weights.reshape(layers, -1, channels), point_weights)


def teacher_kernel(
    rows_each, total_rows, parts_ref, weights_ref, last_ref, project_ref, wide_ref, narrow_ref,
    kernel_ref, active_ref, sum_ref, copy_sems,
):
    slots, own_frames, rows, width, channels = parts_ref.shape
    frames = slots * own_frames
    padded = kernel_ref.shape[3] // 3
    time, _, _, first_row = row_position(rows_each)

    def copies(conv):
        return [
            pltpu.make_async_copy(
                weights_ref.at[conv, :, side],
                kernel_ref.at[conv, :, 0, pl.ds(side * padded, channels), :],
                copy_sems.at[conv, side],
            )
            for side in range(3)
        ]

    for conv in range(2):
        for copy in copies(conv):
            copy.start()
    for conv in range(2):
        for side in range(3):
            kernel_ref[conv, :, 0, side * padded + channels : (side + 1) * padded, :] = jnp.zeros(
                (9, padded - channels, channels), jnp.bfloat16
            )

    active_ref[...] = jnp.zeros(active_ref.shape, jnp.bfloat16)

    def source(t):
        return slot_of(t // own_frames, time, slots), t % own_frames

    def spread_columns(t, row, value):
        for side in range(3):
            piece = value if side == 1 else moved(value, 1 - side)
            active_ref[t + FRAME_REACH, row, :, side * padded : side * padded + channels] = (
                piece.astype(jnp.bfloat16)
            )

    def activated(value):
        mean = jnp.mean(value * value, axis=-1, keepdims=True)
        normed = value * lax.rsqrt(mean + 1e-06)
        return (normed * jax.nn.sigmoid(normed)).astype(jnp.bfloat16).astype(jnp.float32)

    def first(t, carry):
        slot, frame = source(t)
        for row in range(rows):
            spread_columns(t, row, activated(parts_ref[slot, frame, row].astype(jnp.float32)))
        return carry

    lax.fori_loop(0, frames, first, 0)

    def convolve(conv, out_rows):
        def tap(index, carry):
            step_t, step_h = index // 3, index % 3
            field = active_ref[pl.ds(step_t, frames), pl.ds(step_h, out_rows)]
            term = jnp.dot(
                field.reshape(frames * out_rows * width, 3 * padded),
                kernel_ref[conv, index, 0],
                preferred_element_type=jnp.float32,
            )

            @pl.when(index == 0)
            def _():
                sum_ref[0 : frames * out_rows * width] = term

            @pl.when(index > 0)
            def _():
                sum_ref[0 : frames * out_rows * width] += term

            return carry

        for copy in copies(conv):
            copy.wait()
        lax.fori_loop(0, 9, tap, 0)

    convolve(0, rows - 2)

    def second(t, carry):
        for row in range(rows - 2):
            base = (t * (rows - 2) + row) * width
            value = sum_ref[pl.ds(pl.multiple_of(base, width), width), :]
            spread_columns(
                t, row, activated(value) * row_mask(first_row + row - 1, total_rows)
            )
        return carry

    lax.fori_loop(0, frames, second, 0)
    convolve(1, rows - 4)

    def finish(t, carry):
        slot, frame = source(t)
        count = rows_each * width
        summed = sum_ref[pl.ds(pl.multiple_of(t * count, count), count), :]
        field = parts_ref[slot, frame, 2 : 2 + rows_each].astype(jnp.float32)
        target = (field.reshape(count, channels) + summed).astype(jnp.bfloat16)
        projected = jnp.dot(
            last_ref[t].reshape(count, -1), project_ref[...], preferred_element_type=jnp.float32
        )
        mismatch = (projected - target.astype(jnp.float32)).astype(jnp.bfloat16)
        gradient = lax.dot_general(
            mismatch, project_ref[...], (((1,), (1,)), ((), ())),
            preferred_element_type=jnp.float32,
        ).reshape(rows_each, width, -1)
        wide_ref[t] = gradient
        narrow_ref[t] = gradient.astype(jnp.bfloat16)
        return carry

    lax.fori_loop(0, frames, finish, 0)


def teacher_gradient(parts, weights, last, project_weight, rows_each, total_rows):
    slots, own_frames, rows, width, channels = parts.shape
    frames = slots * own_frames
    padded = -(-channels // 128) * 128
    student = last.shape[-1]
    whole = pl.BlockSpec(memory_space=pltpu.VMEM)
    shape = (frames, rows_each, width, student)
    return pl.pallas_call(
        functools.partial(teacher_kernel, rows_each, total_rows),
        out_shape=[
            jax.ShapeDtypeStruct(shape, jnp.float32),
            jax.ShapeDtypeStruct(shape, jnp.bfloat16),
        ],
        in_specs=[whole, pl.BlockSpec(memory_space=pl.ANY), whole, whole],
        scratch_shapes=[
            pltpu.VMEM((2, 9, 1, 3 * padded, channels), jnp.bfloat16),
            pltpu.VMEM((frames + FRAME_REACH, rows, width, 3 * padded), jnp.bfloat16),
            pltpu.VMEM((frames * (rows - 2) * width, channels), jnp.float32),
            pltpu.SemaphoreType.DMA((2, 3)),
        ],
        compiler_params=pltpu.CompilerParams(vmem_limit_bytes=VMEM_BYTES),
        name="teacher_gradient",
    )(parts, weights.reshape(2, 9, 3, channels, channels), last, project_weight)


def backward_kernel(
    rows_each, total_rows, layers, wide_ref, low_ref, high_ref, depth_ref, point_ref, *refs
):
    slope_refs = refs[:layers]
    out_ref, grad_ref, back_ref = refs[layers:]
    frames, _, width, channels = wide_ref.shape
    _, _, _, first_row = row_position(rows_each)
    grad_ref[:, 0:layers] = low_ref[...].astype(jnp.float32)
    grad_ref[:, layers : layers + rows_each] = wide_ref[...]
    grad_ref[:, layers + rows_each :] = high_ref[...].astype(jnp.float32)
    back_ref[frames:] = jnp.zeros((FRAME_REACH,) + back_ref.shape[1:], jnp.float32)
    for layer in reversed(range(layers)):
        shift = layers - (layer + 1)
        count = rows_each + 2 * (layer + 1)

        def unmix(t, carry, shift=shift, count=count, layer=layer):
            gradient = grad_ref[t, shift : shift + count].astype(jnp.bfloat16)
            backward = lax.dot_general(
                gradient.reshape(count * width, channels),
                point_ref[layer],
                (((1,), (1,)), ((), ())),
                preferred_element_type=jnp.float32,
            ).astype(jnp.bfloat16).astype(jnp.float32).reshape(count, width, channels)
            for row in range(count):
                back_ref[t, shift + row] = backward[row] * row_mask(
                    first_row + row - (layer + 1), total_rows
                )
            return carry

        lax.fori_loop(0, frames, unmix, 0)

        def step(t, carry, shift=shift, count=count, layer=layer):
            taps = load_taps(depth_ref, layer)
            for row in range(count - 2):
                spread = tap_sum(
                    lambda i, j, row=row: back_ref[t + i, shift + row + j], taps, True
                )
                value = grad_ref[t, shift + 1 + row] + spread * slope_refs[layer][t, row]
                if layer == 0:
                    out_ref[t, row] = value.astype(jnp.bfloat16)
                else:
                    grad_ref[t, shift + 1 + row] = value
            return carry

        lax.fori_loop(0, frames, step, 0)


def student_backward(
    wide, low, high, depth_weights, point_weights, slopes, rows_each, total_rows
):
    layers = depth_weights.shape[0]
    frames, _, width, channels = wide.shape
    rows = rows_each + 2 * layers
    return pl.pallas_call(
        functools.partial(backward_kernel, rows_each, total_rows, layers),
        out_shape=jax.ShapeDtypeStruct(wide.shape, jnp.bfloat16),
        scratch_shapes=[
            pltpu.VMEM((frames, rows, width, channels), jnp.float32),
            pltpu.VMEM((frames + FRAME_REACH, rows, width, channels), jnp.float32),
        ],
        compiler_params=pltpu.CompilerParams(vmem_limit_bytes=VMEM_BYTES),
        name="student_backward",
    )(wide, low, high, depth_weights.reshape(layers, -1, channels), point_weights, *slopes)


AXES = ("ta", "ha", "wa")


def whole_route(sizes, move):
    times, heights, widths = sizes
    route = []
    for time in range(times):
        for height in range(heights):
            for side in range(widths):
                target = move(time, height, side)
                if target is None:
                    continue
                goal, up, across = target
                if 0 <= up < heights:
                    route.append(
                        (
                            (time * heights + height) * widths + side,
                            (goal * heights + up) * widths + across,
                        )
                    )
    return route


def chain_swap(parity, widths, longest):
    def move(time, height, side):
        chain = height * widths + side
        other = chain + 1 if chain % 2 == parity else chain - 1
        if not 0 <= other < longest:
            return None
        return time, other // widths, other % widths

    return move


def rows_of(block, begin, count, axis):
    return lax.dynamic_slice_in_dim(block, begin, count, axis=axis)


def over_time(block, halo, rows_each):
    time, _, part, _ = row_position(rows_each)
    count = lax.axis_size("ta")
    parts = block[None]
    distance = count // 2
    while distance:
        rows = rows_each * distance + 2 * halo
        upper = (part // distance) % 2
        kept = rows_of(parts, upper * rows_each * distance, rows, 2)
        sent = rows_of(parts, (1 - upper) * rows_each * distance, rows, 2)
        got = lax.ppermute(sent, "ta", [(i, i ^ distance) for i in range(count)])
        parts = jnp.concatenate([kept, got], axis=0)
        distance //= 2
    return parts


def gather_student(block, halo, rows_each, sizes):
    _, chain, _, _ = row_position(rows_each)
    rows = block.shape[1]
    longest = sizes[1] * sizes[2]
    even = chain % 2 == 0
    start = jnp.where(even, rows - halo, 0)
    swap_even = lax.ppermute(
        rows_of(block, start, halo, 1), AXES, whole_route(sizes, chain_swap(0, sizes[2], longest))
    )
    swap_odd = lax.ppermute(
        rows_of(block, rows - halo - start, halo, 1),
        AXES,
        whole_route(sizes, chain_swap(1, sizes[2], longest)),
    )
    low = jnp.where(even, swap_odd, swap_even)
    high = jnp.where(even, swap_even, swap_odd)
    return over_time(jnp.concatenate([low, block, high], axis=1), halo, rows_each)


def gather_teacher(tile, halo, rows_each, sizes):
    side = lax.axis_index("wa")
    rows = tile.shape[1] // 2
    left = side == 0

    def for_side(which):
        block = rows_of(tile, which * (rows - halo), rows + halo, 1)
        edge = rows_of(tile, (1 - which) * (2 * rows - halo), halo, 1)
        return jnp.concatenate([block, edge], axis=1)

    mine = for_side(side)
    other = lax.ppermute(for_side(1 - side), "wa", [(0, 1), (1, 0)])
    full = jnp.concatenate(
        [jnp.where(left, mine, other), jnp.where(left, other, mine)], axis=2
    )
    block, edge = full[:, : rows + halo], full[:, rows + halo :]
    beyond = lax.ppermute(
        edge,
        AXES,
        whole_route(sizes, lambda time, up, across: (time, up + (1 - 2 * across), across)),
    )
    extended = jnp.where(
        left,
        jnp.concatenate([beyond, block], axis=1),
        jnp.concatenate([block, beyond], axis=1),
    )
    return over_time(extended, halo, rows_each)


def gradient_borders(narrow, halo, rows_each, sizes):
    times, heights, widths = sizes
    _, _, part, _ = row_position(rows_each)
    longest = heights * widths
    even = part % 2 == 0

    def place(time, height, side):
        chain = height * widths + side
        return chain * times + (time ^ ((chain & 1) * (times - 1)))

    def swap(parity):
        def move(time, height, side):
            position = place(time, height, side)
            other = position + 1 if position % 2 == parity else position - 1
            if not 0 <= other < longest * times:
                return None
            chain, index = divmod(other, times)
            return index ^ ((chain & 1) * (times - 1)), chain // widths, chain % widths

        return whole_route(sizes, move)

    top = narrow[:, narrow.shape[1] - halo :]
    bottom = narrow[:, :halo]
    outer = lax.ppermute(jnp.where(even, bottom, top), AXES, swap(1))
    inner = lax.ppermute(jnp.where(even, top, bottom), AXES, swap(0))
    return jnp.where(even, outer, inner), jnp.where(even, inner, outer)


def give_back(out, rows_each):
    time, _, part, _ = row_position(rows_each)
    count = lax.axis_size("ta")
    frames = out.shape[0] // count
    pieces = []
    for difference in range(count):
        sent = rows_of(out, (time ^ difference) * frames, frames, 0)
        if difference:
            sent = lax.ppermute(sent, "ta", [(i, i ^ difference) for i in range(count)])
        pieces.append(sent)
    stacked = jnp.stack(pieces)
    ordered = [
        lax.dynamic_index_in_dim(stacked, part ^ index, 0, keepdims=False)
        for index in range(count)
    ]
    return jnp.concatenate(ordered, axis=1)


def gathered(sizes, total_rows):
    rows_each = total_rows // (sizes[0] * sizes[1] * sizes[2])

    def on_device_gathered(
        teacher_in, teacher_weights, student_in, depth_weights, point_weights, project_weight
    ):
        layers = depth_weights.shape[0]
        halo = student_halos(layers)[0]
        student_parts = gather_student(student_in, halo, rows_each, sizes)
        teacher_parts = gather_teacher(teacher_in, TEACHER_HALO, rows_each, sizes)
        last, *slopes = student_forward(
            student_parts, depth_weights, point_weights, rows_each, total_rows
        )
        wide, narrow = teacher_gradient(
            teacher_parts, teacher_weights[0], last, project_weight, rows_each, total_rows
        )
        low, high = gradient_borders(narrow, layers, rows_each, sizes)
        out = student_backward(
            wide, low, high, depth_weights, point_weights, slopes, rows_each, total_rows
        )
        return give_back(out, rows_each)

    return on_device_gathered


def can_gather(sizes, shape_rows, width, layers):
    times, heights, widths = sizes
    block = shape_rows // (heights * widths)
    return (
        widths == 2
        and times & (times - 1) == 0
        and block % times == 0
        and block // times >= max(layers, TEACHER_HALO)
        and block >= student_halos(layers)[0]
        and width % 16 == 0
    )


def from_behind(block, axis, distance):
    devices = range(lax.axis_size(axis))
    route = [(i - distance, i) for i in devices if i - distance in devices]
    return lax.ppermute(block, axis, route)


def extended_2(block, sides, width):
    for axis, dim in sides:
        count = lax.axis_size(axis)
        forward = [(i, i + 1) for i in range(count - 1)]
        backward = [(target, source) for source, target in forward]
        low = lax.ppermute(
            lax.slice_in_dim(block, block.shape[dim] - width, None, axis=dim), axis, forward
        )
        high = lax.ppermute(lax.slice_in_dim(block, 0, width, axis=dim), axis, backward)
        block = jnp.concatenate([low, block, high], axis=dim)
    return block


def root_norm(field):
    return field * lax.rsqrt(jnp.mean(field * field, axis=-1, keepdims=True) + 1e-06)


def silu_slope(field):
    sigmoid_value = jax.nn.sigmoid(field)
    return sigmoid_value * (1.0 + field * (1.0 - sigmoid_value))


def dense_conv(extended, kernel):
    frame_count = extended.shape[0] - 2
    row_count = extended.shape[1] - 2
    col_count = extended.shape[2] - 2
    channels = kernel.shape[-1]
    tap_list = []
    for step_t in range(3):
        for step_h in range(3):
            for step_w in range(3):
                tap_list.append(
                    extended[
                        step_t : step_t + frame_count,
                        step_h : step_h + row_count,
                        step_w : step_w + col_count,
                    ]
                )
    stacked = jnp.concatenate(tap_list, axis=-1).reshape(frame_count * row_count * col_count, -1)
    summed = jnp.dot(stacked, kernel.reshape(-1, channels), preferred_element_type=jnp.float32)
    return summed.reshape(frame_count, row_count, col_count, channels)


def depthwise(extended, kernel):
    frame_count = extended.shape[0] - 2
    row_count = extended.shape[1] - 2
    col_count = extended.shape[2] - 2
    summed = jnp.zeros((frame_count, row_count, col_count, kernel.shape[-1]), jnp.float32)
    for step_t in range(3):
        for step_h in range(3):
            for step_w in range(3):
                tap_slice = extended[
                    step_t : step_t + frame_count,
                    step_h : step_h + row_count,
                    step_w : step_w + col_count,
                ]
                summed = summed + tap_slice.astype(jnp.float32) * kernel[step_t, step_h, step_w]
    return summed


def teacher_extend(active):
    earlier = from_behind(active, "ta", 1)
    longer = jnp.concatenate([earlier, active], axis=0)
    return extended_2(longer, (("ha", 1), ("wa", 2)), 1)


def rows_border(longer):
    widened = extended_2(longer, ((("ha", "wa"), 1),), 1)
    return jnp.pad(widened, ((0, 0), (0, 0), (1, 1), (0, 0)))


def rows_extend_past(active):
    earlier = from_behind(active, "ta", 1)
    return rows_border(jnp.concatenate([earlier, active], axis=0))


def rows_extend_future(backward):
    upcoming = from_behind(backward, "ta", -1)
    return rows_border(jnp.concatenate([backward, upcoming], axis=0))


def student_pass(
    initial, target, depth_weights, point_weights, project_weight, extend_past, extend_future
):
    channels = initial.shape[-1]
    current = initial.astype(jnp.float32)
    stored = []
    for layer_index in range(depth_weights.shape[0]):
        active = jax.nn.silu(current).astype(jnp.bfloat16)
        spread = depthwise(extend_past(active), depth_weights[layer_index]).astype(jnp.bfloat16)
        stored.append(current)
        mixed = jnp.dot(
            spread.reshape(-1, channels),
            point_weights[layer_index],
            preferred_element_type=jnp.float32,
        )
        current = current + mixed.reshape(current.shape)
    projected = jnp.dot(
        current.astype(jnp.bfloat16).reshape(-1, channels),
        project_weight,
        preferred_element_type=jnp.float32,
    )
    mismatch = (projected - target.astype(jnp.float32).reshape(projected.shape)).astype(
        jnp.bfloat16
    )
    gradient = lax.dot_general(
        mismatch, project_weight, (((1,), (1,)), ((), ())), preferred_element_type=jnp.float32
    ).reshape(current.shape)
    for layer_index in reversed(range(depth_weights.shape[0])):
        backward = lax.dot_general(
            gradient.astype(jnp.bfloat16).reshape(-1, channels),
            point_weights[layer_index],
            (((1,), (1,)), ((), ())),
            preferred_element_type=jnp.float32,
        )
        backward = backward.astype(jnp.bfloat16).reshape(current.shape)
        flipped = depth_weights[layer_index][::-1, ::-1, ::-1]
        spread_back = depthwise(extend_future(backward), flipped)
        gradient = gradient + spread_back * silu_slope(stored[layer_index])
    return gradient.astype(jnp.bfloat16)


def on_device(
    teacher_in, teacher_weights, student_in, depth_weights, point_weights, project_weight
):
    target = teacher_in
    current = target.astype(jnp.float32)
    active = jax.nn.silu(root_norm(current)).astype(jnp.bfloat16)
    middle = dense_conv(teacher_extend(active), teacher_weights[0, 0])
    second = jax.nn.silu(root_norm(middle)).astype(jnp.bfloat16)
    target = (current + dense_conv(teacher_extend(second), teacher_weights[0, 1])).astype(
        jnp.bfloat16
    )
    regrouped = lax.all_to_all(target, "wa", split_axis=1, concat_axis=2, tiled=True)
    return student_pass(
        student_in,
        regrouped,
        depth_weights,
        point_weights,
        project_weight,
        rows_extend_past,
        rows_extend_future,
    )


def solution(mesh):
    sizes = tuple(mesh.shape[axis] for axis in AXES)
    placed = (P("ta", "ha", "wa", None), P(), P("ta", ("ha", "wa"), None, None), P(), P(), P())

    def whole(
        teacher_in, teacher_weights, student_in, depth_weights, point_weights, project_weight
    ):
        total_rows, width = student_in.shape[1], student_in.shape[2]
        body = on_device
        if can_gather(sizes, total_rows, width, depth_weights.shape[0]):
            body = gathered(sizes, total_rows)
        return jax.shard_map(
            body,
            mesh=mesh,
            in_specs=placed,
            out_specs=P("ta", ("ha", "wa"), None, None),
            check_vma=False,
        )(teacher_in, teacher_weights, student_in, depth_weights, point_weights, project_weight)

    return whole
```
